256 devices in a mesh: src: 16 (over y_lo, z), tgt: 16 (over x, y_hi, core).
Axes of the slice: x: 4, y: 4 (y_hi: 2, y_lo: 2; y = y_hi * 2 + y_lo), z: 8, core: 2. Of those that a mesh axis runs over, the one named last changes fastest.
Arguments:
- coefficients: float32 [2048, 128, 512], P(('src', 'tgt')), may hold values from -6 to 6
- transfer: float32 [8, 2048, 128, 256], P(None, ('src', 'tgt')), may hold values from -0.375 to 0.375
- local_bits: int32 [4], replicated, may hold values from 0 to 2
- relabel: int32 [1024], replicated, may hold values from 0 to 1023, each once
Outputs:
- result: float32 [2048, 128, 512], P(('src', 'tgt'))
The draws below stay inside these ranges and needn't reach their ends.
Inputs may be any that keep to these rules, and one draw needn't show every extreme that they name: `local_bits`: each entry names a bit of a node's position among the 8 nodes of one device. `relabel`: a permutation of the 1024 rows of one device.
All inputs are finite; a program needn't handle non-finite values.
Results may differ from the reference program's by a relative error of at most 0.00007.
Values sent between devices are 32-bit elements; how exact they have to be, the bound alone decides.
A program may use at most 64 MiB of HBM per device.

```python
import jax
import jax.numpy as jnp
from jax import lax

NODE_BITS = 3
NODES_DEV = 8
RANK = 128
RHS = 512
LOCAL_LEVELS = 4
LEVELS = 8
ROWS_DEV = 1024
NODES = 2048
N_SRC = 16
N_TGT = 16


def place_ends(array, stream_key, least, top_value):
    dims = array.shape
    index_at = [jax.random.randint(jax.random.fold_in(stream_key, axis), (), 0, dims[axis]) for axis in range(len(dims))]
    array = array.at[tuple(index_at)].set(least)
    longest = dims.index(max(dims))
    index_at[longest] = (index_at[longest] + 1) % dims[longest]
    return array.at[tuple(index_at)].set(top_value)


def levels(key, extent, split, low, largest):
    factor_of, own = 1.0, jax.random.fold_in(key, 6)
    for position, parts in split:
        draws = jnp.exp(jax.random.uniform(jax.random.fold_in(own, position), (parts,), jnp.float32, low / len(split), largest / len(split)))
        factor_of = factor_of * jnp.repeat(draws, extent[position] // parts).reshape([-1 if axis == position else 1 for axis in range(len(extent))])
    return factor_of


def bell_draw(own_key, dims, deviation, limit, shards=(), kind=jnp.bfloat16):
    loudness = levels(own_key, dims, shards, -0.22, 0.18) if shards else 1.0
    array = jax.random.normal(own_key, dims, jnp.float32) * deviation * loudness
    return jnp.minimum(jnp.maximum(array, -limit), limit).astype(kind)


def setup_inputs(seed: int = 0) -> dict:
    seeds = jax.random.split(jax.random.key(seed), 5)
    coefficients = bell_draw(seeds[0], (NODES, RANK, RHS), 1.0, 6.0, ((0, 256),), jnp.float32)
    transfer = bell_draw(seeds[1], (LEVELS, NODES, RANK, 2 * RANK), (2 * RANK) ** -0.5, 0.375, ((1, 256),), jnp.float32)
    local_bits = place_ends(jax.random.randint(seeds[2], (LOCAL_LEVELS,), 0, NODE_BITS), jax.random.fold_in(seeds[2], 1), 0, NODE_BITS - 1).astype(jnp.int32)
    relabel = jax.random.permutation(seeds[3], ROWS_DEV).astype(jnp.int32)
    return dict(coefficients=coefficients, transfer=transfer, local_bits=local_bits, relabel=relabel)


def combine(node_state, partner_state, transfer_block, lower_side):
    rank_width = node_state.shape[1]
    leading = jnp.where(lower_side, node_state, partner_state)
    trailing = jnp.where(lower_side, partner_state, node_state)
    first_part = jnp.einsum("nrk,nkc->nrc", transfer_block[:, :, :rank_width], leading, precision=lax.Precision.HIGHEST)
    second_part = jnp.einsum("nrk,nkc->nrc", transfer_block[:, :, rank_width:], trailing, precision=lax.Precision.HIGHEST)
    return first_part + second_part


def pair_level(node_state, transfer_block, distance):
    node_index = jnp.arange(node_state.shape[0], dtype=jnp.int32)
    distance = jnp.asarray(distance, dtype=jnp.int32)
    partner = jnp.bitwise_xor(node_index, distance).astype(jnp.int32)
    lower_side = (jnp.bitwise_and(node_index, distance) == 0)[:, None, None]
    partner_state = jnp.take(node_state, partner, axis=0)
    return combine(node_state, partner_state, transfer_block, lower_side)


def local_distance(local_bits, slot_index):
    return jnp.left_shift(jnp.int32(1), local_bits[slot_index]).astype(jnp.int32)


def reference(coefficients, transfer, local_bits, relabel):
    node_state = pair_level(coefficients, transfer[0], local_distance(local_bits, 0))
    node_state = pair_level(node_state, transfer[1], (N_SRC // 2) * N_TGT * NODES_DEV)
    node_state = pair_level(node_state, transfer[2], local_distance(local_bits, 1))
    node_state = pair_level(node_state, transfer[3], N_TGT * NODES_DEV)
    columns = node_state.shape[2]
    blocks = node_state.reshape(N_SRC, N_TGT, ROWS_DEV, columns)
    blocks = jnp.take(blocks, relabel.astype(jnp.int32), axis=2)
    blocks = blocks.reshape(N_SRC, N_TGT, N_TGT, ROWS_DEV // N_TGT, columns)
    blocks = jnp.swapaxes(blocks, 1, 2)
    node_state = blocks.reshape(NODES, RANK, columns)
    node_state = pair_level(node_state, transfer[4], (N_TGT // 2) * NODES_DEV)
    node_state = pair_level(node_state, transfer[5], local_distance(local_bits, 2))
    node_state = pair_level(node_state, transfer[6], NODES_DEV)
    node_state = pair_level(node_state, transfer[7], local_distance(local_bits, 3))
    return node_state
```

```python
import jax
import jax.numpy as jnp
from jax import lax
from jax.experimental import pallas as pl
from jax.experimental.pallas import tpu as pltpu
from jax.sharding import PartitionSpec as P

MESH = pl.DeviceIdType.MESH
F32 = jnp.float32
BF16 = jnp.bfloat16
CHUNKS = 4
WIDTH = 128
RANK = 128
NODES = 8
HALF = 4


def flip(index, mask):
    for bit in (1, 2, 4, 8):
        if mask & bit:
            index = index + bit - 2 * bit * (lax.div(index, bit) % 2)
    return index


def pick(bit, options):
    return jnp.where(bit == 0, options[0], jnp.where(bit == 1, options[1], options[2]))


def bits_of(number):
    return (number >> 2) & 1, (number >> 1) & 1, number & 1


def slot_node(slot, bit):
    a, b, e = bits_of(slot)
    return pick(bit, (4 * a + 2 * b + e, 4 * a + 2 * e + b, 4 * e + 2 * a + b))


def node_slot(node, bit):
    c, b, a = bits_of(node)
    return pick(bit, (4 * c + 2 * b + a, 4 * c + 2 * a + b, 4 * b + 2 * a + c))


def lower(node, bit):
    return pick(bit, (node & ~1, node & ~2, node & ~4))


def upper(node, bit):
    return pick(bit, (node | 1, node | 2, node | 4))


def split(value):
    high = value.astype(BF16)
    low = (value - high.astype(F32)).astype(BF16)
    return jnp.concatenate([high, low], axis=1)


def product(block, state):
    full = jnp.dot(block, state, preferred_element_type=F32)
    both = full[:, :WIDTH] + full[:, WIDTH:]
    return [both[r : r + RANK] + both[r + RANK : r + 2 * RANK] for r in range(0, both.shape[0], 2 * RANK)]


def stack(first, second):
    return jnp.concatenate([first, second], axis=0)


def kernel(
    bits, relabel, coef_hbm, g_hbm, out_hbm,
    x0, graw0, graw, gpart, gb, xa, xc, xe, xf, onehot,
    s0, r1, s2, r3, pm, mid, t4, s4, s5, r6, out,
    tab, in_sem, gs_sem, gr_sem,
    send1, recv1, send3, recv3, sendm, recvm, send4, recv4, send6, recv6, out_sem,
):
    src = lax.axis_index("src")
    tgt = lax.axis_index("tgt")
    far = lax.div(tgt, 8)
    near = tgt % 8
    peer1 = (flip(src, 8), tgt)
    peer3 = (flip(src, 1), tgt)
    peer4 = (src, flip(tgt, 8))
    peer6 = (src, flip(tgt, 1))
    side1 = lax.div(src, 8)
    side3 = src % 2
    side6 = tgt % 2

    barrier = pltpu.get_barrier_semaphore()
    peers = [peer1, peer3, peer4] + [(src, flip(tgt, i)) for i in range(1, 8)]
    for peer in peers:
        pl.semaphore_signal(barrier, inc=1, device_id=peer, device_id_type=MESH)

    load_x = pltpu.make_async_copy(coef_hbm, x0, in_sem.at[0])
    load_g0 = pltpu.make_async_copy(g_hbm.at[0], graw0, in_sem.at[1])
    load_g = pltpu.make_async_copy(g_hbm.at[pl.ds(1, 7)], graw, in_sem.at[2])
    load_g0.start()
    load_x.start()
    load_g.start()

    b0, b1, b2, b3 = bits[0], bits[1], bits[2], bits[3]
    for n in range(NODES):
        nu = slot_node(n, b1)
        tab[0, n] = nu
        tab[1, n] = lower(nu, b0)
        tab[2, n] = upper(nu, b0)
        tab[3, n] = slot_node(n, b2)
        tab[4, n] = node_slot(lower(n, b3), b2)
        tab[5, n] = node_slot(upper(n, b3), b2)

    def remote(source, target, send, recv, peer):
        return pltpu.make_async_remote_copy(
            src_ref=source, dst_ref=target, send_sem=send, recv_sem=recv, device_id=peer, device_id_type=MESH
        )

    def copy1(c, s):
        return remote(s0.at[c, s], r1.at[c, s], send1.at[c, s], recv1.at[c, s], peer1)

    def copy3(c, s):
        return remote(s2.at[c, s], r3.at[c, s], send3.at[c, s], recv3.at[c, s], peer3)

    def copym(c, i):
        q = flip(near, i)
        return remote(
            pm.at[c, :, q], mid.at[c, :, near], sendm.at[c, i], recvm.at[c, i], (src, flip(tgt, i))
        )

    def copy4(c, n):
        return remote(t4.at[c, n], s4.at[c, HALF * far + n], send4.at[c, n], recv4.at[c, n], peer4)

    def copy6(c, s):
        return remote(s5.at[c, s], r6.at[c, s], send6.at[c, s], recv6.at[c, s], peer6)

    def copyg():
        return remote(g_hbm.at[4, pl.ds(HALF * (1 - far), HALF)], gpart, gs_sem, gr_sem, peer4)

    def copyo(c):
        return pltpu.make_async_copy(
            out.at[c], out_hbm.at[:, :, pl.ds(pl.multiple_of(c * WIDTH, WIDTH), WIDTH)], out_sem.at[c]
        )

    def convert(level, slot, first, second):
        for half, block in ((0, first), (1, second)):
            high = block.astype(BF16)
            gb[level, slot, :RANK, half * RANK : (half + 1) * RANK] = high
            gb[level, slot, RANK:, half * RANK : (half + 1) * RANK] = (block - high.astype(F32)).astype(BF16)

    load_g0.wait()
    for s in range(NODES):
        block = graw0[tab[0, s]]
        convert(0, s, block[:, :RANK], block[:, RANK:])
    load_x.wait()
    pl.semaphore_wait(barrier, len(peers))
    copyg().start()

    def phase_a(c, carry):
        columns = pl.ds(pl.multiple_of(c * WIDTH, WIDTH), WIDTH)
        for n in range(NODES):
            xa[n] = split(x0[n, :, columns])
        for s in range(NODES):
            (y,) = product(gb[0, s], stack(xa[tab[1, s]], xa[tab[2, s]]))
            s0[c, s] = y
            copy1(c, s).start()
        return carry

    lax.fori_loop(0, CHUNKS, phase_a, 0)

    load_g.wait()

    def convert_slot(s, carry):
        for level, row in ((2, 0), (5, 3)):
            block = graw[level - 1, tab[row, s]]
            convert(level, s, block[:, :RANK], block[:, RANK:])
        block = graw[6, s]
        convert(7, s, block[:, :RANK], block[:, RANK:])
        for level, row, side in ((1, 0, side1), (3, 0, side3), (6, 3, side6)):
            first = graw[level - 1, tab[row, s], :, pl.ds(pl.multiple_of(side * RANK, RANK), RANK)]
            second = graw[level - 1, tab[row, s], :, pl.ds(pl.multiple_of((1 - side) * RANK, RANK), RANK)]
            convert(level, s, first, second)
        return carry

    lax.fori_loop(0, NODES, convert_slot, 0)

    rows = relabel[...]
    node, row = rows >> 7, rows & 127
    position = (node_slot(node, b1) * RANK + row).astype(F32)
    lanes = lax.broadcasted_iota(jnp.int32, (RANK, RANK), 1).astype(F32)
    for q in range(NODES):
        wanted = jnp.broadcast_to(position[q : q + 1, :], (RANK, RANK)).T
        for k in range(NODES):
            onehot[q * RANK : (q + 1) * RANK, k * RANK : (k + 1) * RANK] = jnp.where(
                wanted == lanes + float(k * RANK), 1.0, 0.0
            ).astype(BF16)

    copyg().wait_recv()
    for n in range(HALF):
        block = graw[3, HALF * far + n]
        convert(4, 2 * n, block[:, :RANK], block[:, RANK:])
        block = gpart[n]
        convert(4, 2 * n + 1, block[:, :RANK], block[:, RANK:])

    def phase_b(c):
        for i in range(HALF):
            parts = []
            for s in (2 * i, 2 * i + 1):
                copy1(c, s).wait_recv()
                (y,) = product(gb[1, s], stack(split(s0[c, s]), split(r1[c, s])))
                parts.append(split(y))
            ys = product(gb[2, 2 * i : 2 * i + 2].reshape(4 * RANK, 2 * RANK), stack(*parts))
            for s, y in zip((2 * i, 2 * i + 1), ys):
                s2[c, s] = y
                copy3(c, s).start()

    def phase_c(c):
        for s in range(NODES):
            copy3(c, s).wait_recv()
            (y,) = product(gb[3, s], stack(split(s2[c, s]), split(r3[c, s])))
            xc[s * RANK : (s + 1) * RANK, :] = split(y)
        state = xc[...]
        for q in range(4):
            full = jnp.dot(onehot[q * 256 : (q + 1) * 256, :], state, preferred_element_type=F32)
            picked = full[:, :WIDTH] + full[:, WIDTH:]
            for k in range(4):
                t = 4 * q + k
                pm[c, t // 8, t % 8] = picked[k * 64 : (k + 1) * 64]
        for i in range(1, 8):
            copym(c, i).start()
        mid[c, 0, near] = pm[c, 0, near]
        mid[c, 1, near] = pm[c, 1, near]

    def phase_d(c):
        for i in range(1, 8):
            copym(c, i).wait_recv()
        for n in range(HALF):
            parts = [split(mid[c, e, 2 * n : 2 * n + 2].reshape(RANK, WIDTH)) for e in range(2)]
            own, other = product(gb[4, 2 * n : 2 * n + 2].reshape(4 * RANK, 2 * RANK), stack(*parts))
            t4[c, n] = other
            copy4(c, n).start()
            s4[c, HALF * far + n] = own

    def phase_e(c):
        for n in range(HALF):
            copy4(c, n).wait_recv()
        for n in range(NODES):
            xe[n] = split(s4[c, n])
        for i in range(HALF):
            state = stack(xe[tab[3, 2 * i]], xe[tab[3, 2 * i + 1]])
            ys = product(gb[5, 2 * i : 2 * i + 2].reshape(4 * RANK, 2 * RANK), state)
            for s, y in zip((2 * i, 2 * i + 1), ys):
                s5[c, s] = y
                copy6(c, s).start()

    def phase_f(c):
        for s in range(NODES):
            copy6(c, s).wait_recv()
            (y,) = product(gb[6, s], stack(split(s5[c, s]), split(r6[c, s])))
            xf[s] = split(y)
        for n in range(NODES):
            (y,) = product(gb[7, n], stack(xf[tab[4, n]], xf[tab[5, n]]))
            out[c, n] = y
        copyo(c).start()

    def step(k, carry):
        for delay, phase in ((0, phase_b), (1, phase_c), (4, phase_d), (5, phase_e), (6, phase_f)):

            @pl.when(jnp.logical_and(k >= delay, k < delay + CHUNKS))
            def _(delay=delay, phase=phase):
                phase(k - delay)

        return carry

    lax.fori_loop(0, CHUNKS + 6, step, 0)

    copyg().wait_send()

    def finish(c, carry):
        for s in range(NODES):
            copy1(c, s).wait_send()
            copy3(c, s).wait_send()
            copy6(c, s).wait_send()
        for i in range(1, 8):
            copym(c, i).wait_send()
        for n in range(HALF):
            copy4(c, n).wait_send()
        copyo(c).wait()
        return carry

    lax.fori_loop(0, CHUNKS, finish, 0)


def on_device(coefficients, transfer, local_bits, relabel):
    state = (CHUNKS, NODES, RANK, WIDTH)
    halves = (CHUNKS, 2, 8, 64, WIDTH)
    dma = pltpu.SemaphoreType.DMA
    return pl.pallas_call(
        kernel,
        out_shape=jax.ShapeDtypeStruct(coefficients.shape, F32),
        in_specs=[
            pl.BlockSpec(memory_space=pltpu.SMEM),
            pl.BlockSpec(memory_space=pltpu.VMEM),
            pl.BlockSpec(memory_space=pl.ANY),
            pl.BlockSpec(memory_space=pl.ANY),
        ],
        out_specs=pl.BlockSpec(memory_space=pl.ANY),
        scratch_shapes=[
            pltpu.VMEM((NODES, RANK, CHUNKS * WIDTH), F32),
            pltpu.VMEM((NODES, RANK, 2 * RANK), F32),
            pltpu.VMEM((7, NODES, RANK, 2 * RANK), F32),
            pltpu.VMEM((HALF, RANK, 2 * RANK), F32),
            pltpu.VMEM((8, NODES, 2 * RANK, 2 * RANK), BF16),
            pltpu.VMEM((NODES, RANK, 2 * WIDTH), BF16),
            pltpu.VMEM((NODES * RANK, 2 * WIDTH), BF16),
            pltpu.VMEM((NODES, RANK, 2 * WIDTH), BF16),
            pltpu.VMEM((NODES, RANK, 2 * WIDTH), BF16),
            pltpu.VMEM((NODES * RANK, NODES * RANK), BF16),
            pltpu.VMEM(state, F32),
            pltpu.VMEM(state, F32),
            pltpu.VMEM(state, F32),
            pltpu.VMEM(state, F32),
            pltpu.VMEM(halves, F32),
            pltpu.VMEM(halves, F32),
            pltpu.VMEM((CHUNKS, HALF, RANK, WIDTH), F32),
            pltpu.VMEM(state, F32),
            pltpu.VMEM(state, F32),
            pltpu.VMEM(state, F32),
            pltpu.VMEM(state, F32),
            pltpu.SMEM((6, NODES), jnp.int32),
            dma((3,)),
            dma,
            dma,
            dma((CHUNKS, NODES)),
            dma((CHUNKS, NODES)),
            dma((CHUNKS, NODES)),
            dma((CHUNKS, NODES)),
            dma((CHUNKS, NODES)),
            dma((CHUNKS, NODES)),
            dma((CHUNKS, HALF)),
            dma((CHUNKS, HALF)),
            dma((CHUNKS, NODES)),
            dma((CHUNKS, NODES)),
            dma((CHUNKS,)),
        ],
        compiler_params=pltpu.CompilerParams(
            collective_id=1, has_side_effects=True, vmem_limit_bytes=60 * 2**20
        ),
    )(local_bits, relabel.reshape(8, 128), coefficients, transfer)


def solution(mesh):
    placed = (P(("src", "tgt"), None, None), P(None, ("src", "tgt"), None, None), P(), P())
    return jax.shard_map(
        on_device,
        mesh=mesh,
        in_specs=placed,
        out_specs=P(("src", "tgt"), None, None),
        check_vma=False,
    )
```

```python
import functools

import jax
import jax.numpy as jnp
from jax import lax
from jax.experimental import pallas as pl
from jax.experimental.pallas import tpu as pltpu
from jax.sharding import PartitionSpec as P

MESH = pl.DeviceIdType.MESH
F32 = jnp.float32
BF16 = jnp.bfloat16
CHUNKS = 4
WIDTH = 128
RANK = 128
NODES = 8
HALF = 4


def flip(index, mask):
    for bit in (1, 2, 4, 8):
        if mask & bit:
            index = index + bit - 2 * bit * (lax.div(index, bit) % 2)
    return index


def pick(bit, options):
    return jnp.where(bit == 0, options[0], jnp.where(bit == 1, options[1], options[2]))


def bits_of(number):
    return (number >> 2) & 1, (number >> 1) & 1, number & 1


def slot_node(slot, bit):
    a, b, e = bits_of(slot)
    return pick(bit, (4 * a + 2 * b + e, 4 * a + 2 * e + b, 4 * e + 2 * a + b))


def node_slot(node, bit):
    c, b, a = bits_of(node)
    return pick(bit, (4 * c + 2 * b + a, 4 * c + 2 * a + b, 4 * b + 2 * a + c))


def lower(node, bit):
    return pick(bit, (node & ~1, node & ~2, node & ~4))


def upper(node, bit):
    return pick(bit, (node | 1, node | 2, node | 4))


def split(value):
    high = value.astype(BF16)
    low = (value - high.astype(F32)).astype(BF16)
    return jnp.concatenate([high, low], axis=1)


def product(block, state):
    full = jnp.dot(block, state, preferred_element_type=F32)
    both = full[:, :WIDTH] + full[:, WIDTH:]
    return [both[r : r + RANK] + both[r + RANK : r + 2 * RANK] for r in range(0, both.shape[0], 2 * RANK)]


def stack(first, second):
    return jnp.concatenate([first, second], axis=0)


def kernel(
    bits, relabel, coef_hbm, g_hbm, out_hbm,
    x0, graw0, graw, gpart, gb, xa, xc, xe, xf, onehot,
    s0, r1, s2, r3, pm, mid, t4, s4, s5, r6, out,
    tab, in_sem, x_sem, gs_sem, gr_sem,
    send1, recv1, send3, recv3, sendm, recvm, send4, recv4, send6, recv6, out_sem,
):
    src = lax.axis_index("src")
    tgt = lax.axis_index("tgt")
    far = lax.div(tgt, 8)
    near = tgt % 8
    spot = [flip(lax.div(near, 2), k) for k in range(HALF)]
    peer1 = (flip(src, 8), tgt)
    peer3 = (flip(src, 1), tgt)
    peer4 = (src, flip(tgt, 8))
    peer6 = (src, flip(tgt, 1))
    side1 = lax.div(src, 8)
    side3 = src % 2
    side6 = tgt % 2

    barrier = pltpu.get_barrier_semaphore()
    peers = [peer1, peer3, peer4] + [(src, flip(tgt, i)) for i in range(1, 8)]
    for peer in peers:
        pl.semaphore_signal(barrier, inc=1, device_id=peer, device_id_type=MESH)

    def copyx(c):
        columns = pl.ds(pl.multiple_of(c * WIDTH, WIDTH), WIDTH)
        return pltpu.make_async_copy(coef_hbm.at[:, :, columns], x0.at[c], x_sem.at[c])

    load_g0 = pltpu.make_async_copy(g_hbm.at[0], graw0, in_sem.at[0])
    load_g = pltpu.make_async_copy(g_hbm.at[pl.ds(1, 7)], graw, in_sem.at[1])
    load_g0.start()
    for c in range(CHUNKS):
        copyx(c).start()

    b0, b1, b2, b3 = bits[0], bits[1], bits[2], bits[3]
    for n in range(NODES):
        nu = slot_node(n, b1)
        tab[0, n] = nu
        tab[1, n] = lower(nu, b0)
        tab[2, n] = upper(nu, b0)
        tab[3, n] = slot_node(n, b2)
        tab[4, n] = node_slot(lower(n, b3), b2)
        tab[5, n] = node_slot(upper(n, b3), b2)

    def remote(source, target, send, recv, peer):
        return pltpu.make_async_remote_copy(
            src_ref=source, dst_ref=target, send_sem=send, recv_sem=recv, device_id=peer, device_id_type=MESH
        )

    def copy1(c, s):
        return remote(s0.at[c, s], r1.at[c, s], send1.at[c, s], recv1.at[c, s], peer1)

    def copy3(c, s):
        return remote(s2.at[c, s], r3.at[c, s], send3.at[c, s], recv3.at[c, s], peer3)

    def copym(c, i):
        q = flip(near, i)
        return remote(
            pm.at[c, :, q], mid.at[c, :, near], sendm.at[c, i], recvm.at[c, i], (src, flip(tgt, i))
        )

    def copy4(c, k):
        return remote(t4.at[c, k], s4.at[c, HALF * far + spot[k]], send4.at[c, k], recv4.at[c, k], peer4)

    def copy6(c, s):
        return remote(s5.at[c, s], r6.at[c, s], send6.at[c, s], recv6.at[c, s], peer6)

    def copyg():
        return remote(g_hbm.at[4, pl.ds(HALF * (1 - far), HALF)], gpart, gs_sem, gr_sem, peer4)

    def copyo(c):
        return pltpu.make_async_copy(
            out.at[c], out_hbm.at[:, :, pl.ds(pl.multiple_of(c * WIDTH, WIDTH), WIDTH)], out_sem.at[c]
        )

    def convert(level, slot, first, second):
        for half, block in ((0, first), (1, second)):
            high = block.astype(BF16)
            gb[level, slot, :RANK, half * RANK : (half + 1) * RANK] = high
            gb[level, slot, RANK:, half * RANK : (half + 1) * RANK] = (block - high.astype(F32)).astype(BF16)

    load_g0.wait()
    for s in range(NODES):
        block = graw0[tab[0, s]]
        convert(0, s, block[:, :RANK], block[:, RANK:])
    load_g.start()
    pl.semaphore_wait(barrier, len(peers))
    copyg().start()

    def phase_a(c, carry):
        copyx(c).wait()
        for n in range(NODES):
            xa[n] = split(x0[c, n])
        for s in range(NODES):
            (y,) = product(gb[0, s], stack(xa[tab[1, s]], xa[tab[2, s]]))
            s0[c, s] = y
            copy1(c, s).start()
        return carry

    lax.fori_loop(0, CHUNKS, phase_a, 0)

    load_g.wait()

    def convert_slot(s, carry):
        for level, row in ((2, 0), (5, 3)):
            block = graw[level - 1, tab[row, s]]
            convert(level, s, block[:, :RANK], block[:, RANK:])
        block = graw[6, s]
        convert(7, s, block[:, :RANK], block[:, RANK:])
        for level, row, side in ((1, 0, side1), (3, 0, side3), (6, 3, side6)):
            first = graw[level - 1, tab[row, s], :, pl.ds(pl.multiple_of(side * RANK, RANK), RANK)]
            second = graw[level - 1, tab[row, s], :, pl.ds(pl.multiple_of((1 - side) * RANK, RANK), RANK)]
            convert(level, s, first, second)
        return carry

    lax.fori_loop(0, NODES, convert_slot, 0)

    rows = relabel[...]
    node, row = rows >> 7, rows & 127
    position = (node_slot(node, b1) * RANK + row).astype(F32)
    lanes = lax.broadcasted_iota(jnp.int32, (RANK, RANK), 1).astype(F32)
    for q in range(NODES):
        wanted = jnp.broadcast_to(position[q : q + 1, :], (RANK, RANK)).T
        for k in range(NODES):
            onehot[q * RANK : (q + 1) * RANK, k * RANK : (k + 1) * RANK] = jnp.where(
                wanted == lanes + float(k * RANK), 1.0, 0.0
            ).astype(BF16)

    copyg().wait_recv()
    for k in range(HALF):
        block = graw[3, HALF * far + spot[k]]
        convert(4, 2 * k, block[:, :RANK], block[:, RANK:])
        block = gpart[spot[k]]
        convert(4, 2 * k + 1, block[:, :RANK], block[:, RANK:])

    def phase_b(c):
        for i in range(HALF):
            parts = []
            for s in (2 * i, 2 * i + 1):
                copy1(c, s).wait_recv()
                (y,) = product(gb[1, s], stack(split(s0[c, s]), split(r1[c, s])))
                parts.append(split(y))
            ys = product(gb[2, 2 * i : 2 * i + 2].reshape(4 * RANK, 2 * RANK), stack(*parts))
            for s, y in zip((2 * i, 2 * i + 1), ys):
                s2[c, s] = y
                copy3(c, s).start()

    def phase_c(c):
        for s in range(NODES):
            copy3(c, s).wait_recv()
            (y,) = product(gb[3, s], stack(split(s2[c, s]), split(r3[c, s])))
            xc[s * RANK : (s + 1) * RANK, :] = split(y)
        state = xc[...]
        for q in range(4):
            full = jnp.dot(onehot[q * 256 : (q + 1) * 256, :], state, preferred_element_type=F32)
            picked = full[:, :WIDTH] + full[:, WIDTH:]
            for k in range(4):
                t = 4 * q + k
                pm[c, t // 8, t % 8] = picked[k * 64 : (k + 1) * 64]
        for i in (6, 7, 4, 5, 2, 3, 1):
            copym(c, i).start()
        mid[c, 0, near] = pm[c, 0, near]
        mid[c, 1, near] = pm[c, 1, near]

    def phase_d(c, order):
        for k in order:
            for i in (2 * k, 2 * k + 1):
                if i:
                    copym(c, i).wait_recv()
            parts = [split(mid[c, e, pl.ds(2 * spot[k], 2)].reshape(RANK, WIDTH)) for e in range(2)]
            own, other = product(gb[4, 2 * k : 2 * k + 2].reshape(4 * RANK, 2 * RANK), stack(*parts))
            t4[c, k] = other
            copy4(c, k).start()
            s4[c, HALF * far + spot[k]] = own

    def phase_e(c):
        for n in range(HALF):
            copy4(c, n).wait_recv()
        for n in range(NODES):
            xe[n] = split(s4[c, n])
        for i in range(HALF):
            state = stack(xe[tab[3, 2 * i]], xe[tab[3, 2 * i + 1]])
            ys = product(gb[5, 2 * i : 2 * i + 2].reshape(4 * RANK, 2 * RANK), state)
            for s, y in zip((2 * i, 2 * i + 1), ys):
                s5[c, s] = y
                copy6(c, s).start()

    def phase_f(c):
        for s in range(NODES):
            copy6(c, s).wait_recv()
            (y,) = product(gb[6, s], stack(split(s5[c, s]), split(r6[c, s])))
            xf[s] = split(y)
        for n in range(NODES):
            (y,) = product(gb[7, n], stack(xf[tab[4, n]], xf[tab[5, n]]))
            out[c, n] = y
        copyo(c).start()

    def step(k, carry):
        for delay, phase in (
            (1, phase_c),
            (0, phase_b),
            (4, functools.partial(phase_d, order=(3, 1))),
            (2, functools.partial(phase_d, order=(0, 2))),
            (5, phase_e),
            (6, phase_f),
        ):

            @pl.when(jnp.logical_and(k >= delay, k < delay + CHUNKS))
            def _(delay=delay, phase=phase):
                phase(k - delay)

        return carry

    lax.fori_loop(0, CHUNKS + 6, step, 0)

    copyg().wait_send()

    def finish(c, carry):
        for s in range(NODES):
            copy1(c, s).wait_send()
            copy3(c, s).wait_send()
            copy6(c, s).wait_send()
        for i in range(1, 8):
            copym(c, i).wait_send()
        for n in range(HALF):
            copy4(c, n).wait_send()
        copyo(c).wait()
        return carry

    lax.fori_loop(0, CHUNKS, finish, 0)


def on_device(coefficients, transfer, local_bits, relabel):
    state = (CHUNKS, NODES, RANK, WIDTH)
    halves = (CHUNKS, 2, 8, 64, WIDTH)
    dma = pltpu.SemaphoreType.DMA
    return pl.pallas_call(
        kernel,
        out_shape=jax.ShapeDtypeStruct(coefficients.shape, F32),
        in_specs=[
            pl.BlockSpec(memory_space=pltpu.SMEM),
            pl.BlockSpec(memory_space=pltpu.VMEM),
            pl.BlockSpec(memory_space=pltpu.HBM),
            pl.BlockSpec(memory_space=pltpu.HBM),
        ],
        out_specs=pl.BlockSpec(memory_space=pl.ANY),
        scratch_shapes=[
            pltpu.VMEM(state, F32),
            pltpu.VMEM((NODES, RANK, 2 * RANK), F32),
            pltpu.VMEM((7, NODES, RANK, 2 * RANK), F32),
            pltpu.VMEM((HALF, RANK, 2 * RANK), F32),
            pltpu.VMEM((8, NODES, 2 * RANK, 2 * RANK), BF16),
            pltpu.VMEM((NODES, RANK, 2 * WIDTH), BF16),
            pltpu.VMEM((NODES * RANK, 2 * WIDTH), BF16),
            pltpu.VMEM((NODES, RANK, 2 * WIDTH), BF16),
            pltpu.VMEM((NODES, RANK, 2 * WIDTH), BF16),
            pltpu.VMEM((NODES * RANK, NODES * RANK), BF16),
            pltpu.VMEM(state, F32),
            pltpu.VMEM(state, F32),
            pltpu.VMEM(state, F32),
            pltpu.VMEM(state, F32),
            pltpu.VMEM(halves, F32),
            pltpu.VMEM(halves, F32),
            pltpu.VMEM((CHUNKS, HALF, RANK, WIDTH), F32),
            pltpu.VMEM(state, F32),
            pltpu.VMEM(state, F32),
            pltpu.VMEM(state, F32),
            pltpu.VMEM(state, F32),
            pltpu.SMEM((6, NODES), jnp.int32),
            dma((2,)),
            dma((CHUNKS,)),
            dma,
            dma,
            dma((CHUNKS, NODES)),
            dma((CHUNKS, NODES)),
            dma((CHUNKS, NODES)),
            dma((CHUNKS, NODES)),
            dma((CHUNKS, NODES)),
            dma((CHUNKS, NODES)),
            dma((CHUNKS, HALF)),
            dma((CHUNKS, HALF)),
            dma((CHUNKS, NODES)),
            dma((CHUNKS, NODES)),
            dma((CHUNKS,)),
        ],
        compiler_params=pltpu.CompilerParams(
            collective_id=1, has_side_effects=True, vmem_limit_bytes=50 * 2**20
        ),
    )(local_bits, relabel.reshape(8, 128), coefficients, transfer)


def solution(mesh):
    placed = (P(("src", "tgt"), None, None), P(None, ("src", "tgt"), None, None), P(), P())
    return jax.shard_map(
        on_device,
        mesh=mesh,
        in_specs=placed,
        out_specs=P(("src", "tgt"), None, None),
        check_vma=False,
    )
```

```python
import functools

import jax
import jax.numpy as jnp
from jax import lax
from jax.experimental import pallas as pl
from jax.experimental.pallas import tpu as pltpu
from jax.sharding import PartitionSpec as P

MESH = pl.DeviceIdType.MESH
F32 = jnp.float32
BF16 = jnp.bfloat16
CHUNKS = 4
WIDTH = 128
RANK = 128
NODES = 8
HALF = 4


def flip(index, mask):
    for bit in (1, 2, 4, 8):
        if mask & bit:
            index = index + bit - 2 * bit * (lax.div(index, bit) % 2)
    return index


def pick(bit, options):
    return jnp.where(bit == 0, options[0], jnp.where(bit == 1, options[1], options[2]))


def bits_of(number):
    return (number >> 2) & 1, (number >> 1) & 1, number & 1


def slot_node(slot, bit):
    a, b, e = bits_of(slot)
    return pick(bit, (4 * a + 2 * b + e, 4 * a + 2 * e + b, 4 * e + 2 * a + b))


def node_slot(node, bit):
    c, b, a = bits_of(node)
    return pick(bit, (4 * c + 2 * b + a, 4 * c + 2 * a + b, 4 * b + 2 * a + c))


def lower(node, bit):
    return pick(bit, (node & ~1, node & ~2, node & ~4))


def upper(node, bit):
    return pick(bit, (node | 1, node | 2, node | 4))


def split(value):
    high = value.astype(BF16)
    low = (value - high.astype(F32)).astype(BF16)
    return jnp.concatenate([high, low], axis=1)


def product(block, state):
    full = jnp.dot(block, state, preferred_element_type=F32)
    both = full[:, :WIDTH] + full[:, WIDTH:]
    return [both[r : r + RANK] + both[r + RANK : r + 2 * RANK] for r in range(0, both.shape[0], 2 * RANK)]


def stack(first, second):
    return jnp.concatenate([first, second], axis=0)


def kernel(
    bits, relabel, coef_hbm, g_hbm, out_hbm,
    x0, graw0, graw, gpart, gb, xa, xc, xe, xf, onehot,
    s0, r1, s2, r3, pm, mid, t4, s4, s5, r6, out,
    tab, in_sem, x_sem, gs_sem, gr_sem,
    send1, recv1, send3, recv3, sendm, recvm, send4, recv4, send6, recv6, out_sem,
):
    src = lax.axis_index("src")
    tgt = lax.axis_index("tgt")
    far = lax.div(tgt, 8)
    near = tgt % 8
    spot = [flip(lax.div(near, 2), k) for k in range(HALF)]
    peer1 = (flip(src, 8), tgt)
    peer3 = (flip(src, 1), tgt)
    peer4 = (src, flip(tgt, 8))
    peer6 = (src, flip(tgt, 1))
    side1 = lax.div(src, 8)
    side3 = src % 2
    side6 = tgt % 2

    barrier = pltpu.get_barrier_semaphore()
    peers = [peer1, peer3, peer4] + [(src, flip(tgt, i)) for i in range(1, 8)]
    for peer in peers:
        pl.semaphore_signal(barrier, inc=1, device_id=peer, device_id_type=MESH)

    def copyx(c):
        columns = pl.ds(pl.multiple_of(c * WIDTH, WIDTH), WIDTH)
        return pltpu.make_async_copy(coef_hbm.at[:, :, columns], x0.at[c], x_sem.at[c])

    load_g0 = pltpu.make_async_copy(g_hbm.at[0], graw0, in_sem.at[0])
    load_g = pltpu.make_async_copy(g_hbm.at[pl.ds(1, 7)], graw, in_sem.at[1])
    load_g0.start()
    for c in range(CHUNKS):
        copyx(c).start()

    b0, b1, b2, b3 = bits[0], bits[1], bits[2], bits[3]
    for n in range(NODES):
        nu = slot_node(n, b1)
        tab[0, n] = nu
        tab[1, n] = lower(nu, b0)
        tab[2, n] = upper(nu, b0)
        tab[3, n] = slot_node(n, b2)
        tab[4, n] = node_slot(lower(n, b3), b2)
        tab[5, n] = node_slot(upper(n, b3), b2)

    def remote(source, target, send, recv, peer):
        return pltpu.make_async_remote_copy(
            src_ref=source, dst_ref=target, send_sem=send, recv_sem=recv, device_id=peer, device_id_type=MESH
        )

    def copy1(c, s):
        return remote(s0.at[c, s], r1.at[c, s], send1.at[c, s], recv1.at[c, s], peer1)

    def copy3(c, s):
        return remote(s2.at[c, s], r3.at[c, s], send3.at[c, s], recv3.at[c, s], peer3)

    def copym(c, i):
        q = flip(near, i)
        return remote(
            pm.at[c, :, q], mid.at[c, :, near], sendm.at[c, i], recvm.at[c, i], (src, flip(tgt, i))
        )

    def copy4(c, k):
        return remote(t4.at[c, k], s4.at[c, HALF * far + spot[k]], send4.at[c, k], recv4.at[c, k], peer4)

    def copy6(c, s):
        return remote(s5.at[c, s], r6.at[c, s], send6.at[c, s], recv6.at[c, s], peer6)

    def copyg():
        return remote(g_hbm.at[4, pl.ds(HALF * (1 - far), HALF)], gpart, gs_sem, gr_sem, peer4)

    def copyo(c):
        return pltpu.make_async_copy(
            out.at[c], out_hbm.at[:, :, pl.ds(pl.multiple_of(c * WIDTH, WIDTH), WIDTH)], out_sem.at[c]
        )

    def convert(level, slot, first, second):
        for half, block in ((0, first), (1, second)):
            high = block.astype(BF16)
            gb[level, slot, :RANK, half * RANK : (half + 1) * RANK] = high
            gb[level, slot, RANK:, half * RANK : (half + 1) * RANK] = (block - high.astype(F32)).astype(BF16)

    load_g0.wait()
    for s in range(NODES):
        block = graw0[tab[0, s]]
        convert(0, s, block[:, :RANK], block[:, RANK:])
    load_g.start()
    pl.semaphore_wait(barrier, len(peers))
    copyg().start()

    def phase_a(c, carry):
        copyx(c).wait()
        for n in range(NODES):
            xa[n] = split(x0[c, n])
        for s in range(NODES):
            (y,) = product(gb[0, s], stack(xa[tab[1, s]], xa[tab[2, s]]))
            s0[c, s] = y
            copy1(c, s).start()
        return carry

    lax.fori_loop(0, CHUNKS, phase_a, 0)

    load_g.wait()

    def convert_slot(s, carry):
        for level, row in ((2, 0), (5, 3)):
            block = graw[level - 1, tab[row, s]]
            convert(level, s, block[:, :RANK], block[:, RANK:])
        block = graw[6, s]
        convert(7, s, block[:, :RANK], block[:, RANK:])
        for level, row, side in ((1, 0, side1), (3, 0, side3), (6, 3, side6)):
            first = graw[level - 1, tab[row, s], :, pl.ds(pl.multiple_of(side * RANK, RANK), RANK)]
            second = graw[level - 1, tab[row, s], :, pl.ds(pl.multiple_of((1 - side) * RANK, RANK), RANK)]
            convert(level, s, first, second)
        return carry

    lax.fori_loop(0, NODES, convert_slot, 0)

    rows = relabel[...]
    node, row = rows >> 7, rows & 127
    position = (node_slot(node, b1) * RANK + row).astype(F32)
    lanes = lax.broadcasted_iota(jnp.int32, (RANK, RANK), 1).astype(F32)
    for q in range(NODES):
        wanted = jnp.broadcast_to(position[q : q + 1, :], (RANK, RANK)).T
        for k in range(NODES):
            onehot[q * RANK : (q + 1) * RANK, k * RANK : (k + 1) * RANK] = jnp.where(
                wanted == lanes + float(k * RANK), 1.0, 0.0
            ).astype(BF16)

    copyg().wait_recv()
    for k in range(HALF):
        block = graw[3, HALF * far + spot[k]]
        convert(4, 2 * k, block[:, :RANK], block[:, RANK:])
        block = gpart[spot[k]]
        convert(4, 2 * k + 1, block[:, :RANK], block[:, RANK:])

    def phase_b(c, pairs):
        for i in pairs:
            parts = []
            for s in (2 * i, 2 * i + 1):
                copy1(c, s).wait_recv()
                (y,) = product(gb[1, s], stack(split(s0[c, s]), split(r1[c, s])))
                parts.append(split(y))
            ys = product(gb[2, 2 * i : 2 * i + 2].reshape(4 * RANK, 2 * RANK), stack(*parts))
            for s, y in zip((2 * i, 2 * i + 1), ys):
                s2[c, s] = y
                copy3(c, s).start()

    def phase_c(c):
        for s in range(NODES):
            copy3(c, s).wait_recv()
            (y,) = product(gb[3, s], stack(split(s2[c, s]), split(r3[c, s])))
            xc[s * RANK : (s + 1) * RANK, :] = split(y)
        state = xc[...]
        for q in range(4):
            full = jnp.dot(onehot[q * 256 : (q + 1) * 256, :], state, preferred_element_type=F32)
            picked = full[:, :WIDTH] + full[:, WIDTH:]
            for k in range(4):
                t = 4 * q + k
                pm[c, t // 8, t % 8] = picked[k * 64 : (k + 1) * 64]
        for i in (4, 5, 6, 7, 2, 3, 1):
            copym(c, i).start()
        mid[c, 0, near] = pm[c, 0, near]
        mid[c, 1, near] = pm[c, 1, near]

    def phase_d(c, order):
        for k in order:
            for i in (2 * k, 2 * k + 1):
                if i:
                    copym(c, i).wait_recv()
            parts = [split(mid[c, e, pl.ds(2 * spot[k], 2)].reshape(RANK, WIDTH)) for e in range(2)]
            own, other = product(gb[4, 2 * k : 2 * k + 2].reshape(4 * RANK, 2 * RANK), stack(*parts))
            t4[c, k] = other
            copy4(c, k).start()
            s4[c, HALF * far + spot[k]] = own

    def phase_e(c):
        for n in range(HALF):
            copy4(c, n).wait_recv()
        for n in range(NODES):
            xe[n] = split(s4[c, n])
        for i in range(HALF):
            state = stack(xe[tab[3, 2 * i]], xe[tab[3, 2 * i + 1]])
            ys = product(gb[5, 2 * i : 2 * i + 2].reshape(4 * RANK, 2 * RANK), state)
            for s, y in zip((2 * i, 2 * i + 1), ys):
                s5[c, s] = y
                copy6(c, s).start()

    def phase_f(c):
        for s in range(NODES):
            copy6(c, s).wait_recv()
            (y,) = product(gb[6, s], stack(split(s5[c, s]), split(r6[c, s])))
            xf[s] = split(y)
        for n in range(NODES):
            (y,) = product(gb[7, n], stack(xf[tab[4, n]], xf[tab[5, n]]))
            out[c, n] = y
        copyo(c).start()

    def step(k, carry):
        for delay, phase in (
            (0, functools.partial(phase_b, pairs=(0, 1))),
            (2, functools.partial(phase_d, order=(3,))),
            (4, functools.partial(phase_d, order=(1,))),
            (1, functools.partial(phase_d, order=(0, 2))),
            (0, functools.partial(phase_b, pairs=(2, 3))),
            (0, phase_c),
            (6, phase_f),
            (5, phase_e),
        ):

            @pl.when(jnp.logical_and(k >= delay, k < delay + CHUNKS))
            def _(delay=delay, phase=phase):
                phase(k - delay)

        return carry

    lax.fori_loop(0, CHUNKS + 6, step, 0)

    copyg().wait_send()

    def finish(c, carry):
        for s in range(NODES):
            copy1(c, s).wait_send()
            copy3(c, s).wait_send()
            copy6(c, s).wait_send()
        for i in range(1, 8):
            copym(c, i).wait_send()
        for n in range(HALF):
            copy4(c, n).wait_send()
        copyo(c).wait()
        return carry

    lax.fori_loop(0, CHUNKS, finish, 0)


def on_device(coefficients, transfer, local_bits, relabel):
    state = (CHUNKS, NODES, RANK, WIDTH)
    halves = (CHUNKS, 2, 8, 64, WIDTH)
    dma = pltpu.SemaphoreType.DMA
    return pl.pallas_call(
        kernel,
        out_shape=jax.ShapeDtypeStruct(coefficients.shape, F32),
        in_specs=[
            pl.BlockSpec(memory_space=pltpu.SMEM),
            pl.BlockSpec(memory_space=pltpu.VMEM),
            pl.BlockSpec(memory_space=pltpu.HBM),
            pl.BlockSpec(memory_space=pltpu.HBM),
        ],
        out_specs=pl.BlockSpec(memory_space=pl.ANY),
        scratch_shapes=[
            pltpu.VMEM(state, F32),
            pltpu.VMEM((NODES, RANK, 2 * RANK), F32),
            pltpu.VMEM((7, NODES, RANK, 2 * RANK), F32),
            pltpu.VMEM((HALF, RANK, 2 * RANK), F32),
            pltpu.VMEM((8, NODES, 2 * RANK, 2 * RANK), BF16),
            pltpu.VMEM((NODES, RANK, 2 * WIDTH), BF16),
            pltpu.VMEM((NODES * RANK, 2 * WIDTH), BF16),
            pltpu.VMEM((NODES, RANK, 2 * WIDTH), BF16),
            pltpu.VMEM((NODES, RANK, 2 * WIDTH), BF16),
            pltpu.VMEM((NODES * RANK, NODES * RANK), BF16),
            pltpu.VMEM(state, F32),
            pltpu.VMEM(state, F32),
            pltpu.VMEM(state, F32),
            pltpu.VMEM(state, F32),
            pltpu.VMEM(halves, F32),
            pltpu.VMEM(halves, F32),
            pltpu.VMEM((CHUNKS, HALF, RANK, WIDTH), F32),
            pltpu.VMEM(state, F32),
            pltpu.VMEM(state, F32),
            pltpu.VMEM(state, F32),
            pltpu.VMEM(state, F32),
            pltpu.SMEM((6, NODES), jnp.int32),
            dma((2,)),
            dma((CHUNKS,)),
            dma,
            dma,
            dma((CHUNKS, NODES)),
            dma((CHUNKS, NODES)),
            dma((CHUNKS, NODES)),
            dma((CHUNKS, NODES)),
            dma((CHUNKS, NODES)),
            dma((CHUNKS, NODES)),
            dma((CHUNKS, HALF)),
            dma((CHUNKS, HALF)),
            dma((CHUNKS, NODES)),
            dma((CHUNKS, NODES)),
            dma((CHUNKS,)),
        ],
        compiler_params=pltpu.CompilerParams(
            collective_id=1, has_side_effects=True, vmem_limit_bytes=50 * 2**20
        ),
    )(local_bits, relabel.reshape(8, 128), coefficients, transfer)


def solution(mesh):
    placed = (P(("src", "tgt"), None, None), P(None, ("src", "tgt"), None, None), P(), P())
    return jax.shard_map(
        on_device,
        mesh=mesh,
        in_specs=placed,
        out_specs=P(("src", "tgt"), None, None),
        check_vma=False,
    )
```

```python
import functools

import jax
import jax.numpy as jnp
from jax import lax
from jax.experimental import pallas as pl
from jax.experimental.pallas import tpu as pltpu
from jax.sharding import PartitionSpec as P

MESH = pl.DeviceIdType.MESH
F32 = jnp.float32
BF16 = jnp.bfloat16
CHUNKS = 4
WIDTH = 128
RANK = 128
NODES = 8
HALF = 4


def flip(index, mask):
    for bit in (1, 2, 4, 8):
        if mask & bit:
            index = index + bit - 2 * bit * (lax.div(index, bit) % 2)
    return index


def pick(bit, options):
    return jnp.where(bit == 0, options[0], jnp.where(bit == 1, options[1], options[2]))


def bits_of(number):
    return (number >> 2) & 1, (number >> 1) & 1, number & 1


def slot_node(slot, bit):
    a, b, e = bits_of(slot)
    return pick(bit, (4 * a + 2 * b + e, 4 * a + 2 * e + b, 4 * e + 2 * a + b))


def node_slot(node, bit):
    c, b, a = bits_of(node)
    return pick(bit, (4 * c + 2 * b + a, 4 * c + 2 * a + b, 4 * b + 2 * a + c))


def lower(node, bit):
    return pick(bit, (node & ~1, node & ~2, node & ~4))


def upper(node, bit):
    return pick(bit, (node | 1, node | 2, node | 4))


def split(value):
    high = value.astype(BF16)
    low = (value - high.astype(F32)).astype(BF16)
    return jnp.concatenate([high, low], axis=1)


def product(block, state):
    full = jnp.dot(block, state, preferred_element_type=F32)
    both = full[:, :WIDTH] + full[:, WIDTH:]
    return [both[r : r + RANK] + both[r + RANK : r + 2 * RANK] for r in range(0, both.shape[0], 2 * RANK)]


def stack(first, second):
    return jnp.concatenate([first, second], axis=0)


def kernel(
    bits, relabel, coef_hbm, g_hbm, out_hbm,
    x0, graw0, graw, gpart, gb, xa, xc, xe, xf, onehot,
    s0, r1, s2, r3, pm, mid, t4, s4, s5, r6, out,
    tab, in_sem, x_sem, gs_sem, gr_sem,
    send1, recv1, send3, recv3, sendm, recvm, send4, recv4, send6, recv6, out_sem,
):
    src = lax.axis_index("src")
    tgt = lax.axis_index("tgt")
    far = lax.div(tgt, 8)
    near = tgt % 8
    spot = [flip(lax.div(near, 2), k) for k in range(HALF)]
    peer1 = (flip(src, 8), tgt)
    peer3 = (flip(src, 1), tgt)
    peer4 = (src, flip(tgt, 8))
    peer6 = (src, flip(tgt, 1))
    side1 = lax.div(src, 8)
    side3 = src % 2
    side6 = tgt % 2

    barrier = pltpu.get_barrier_semaphore()
    peers = [peer1, peer3, peer4] + [(src, flip(tgt, i)) for i in range(1, 8)]
    for peer in peers:
        pl.semaphore_signal(barrier, inc=1, device_id=peer, device_id_type=MESH)

    def copyx(c):
        columns = pl.ds(pl.multiple_of(c * WIDTH, WIDTH), WIDTH)
        return pltpu.make_async_copy(coef_hbm.at[:, :, columns], x0.at[c], x_sem.at[c])

    load_g0 = pltpu.make_async_copy(g_hbm.at[0], graw0, in_sem.at[0])
    load_g = pltpu.make_async_copy(g_hbm.at[pl.ds(1, 7)], graw, in_sem.at[1])
    load_g0.start()
    for c in range(CHUNKS):
        copyx(c).start()

    b0, b1, b2, b3 = bits[0], bits[1], bits[2], bits[3]
    for n in range(NODES):
        nu = slot_node(n, b1)
        tab[0, n] = nu
        tab[1, n] = lower(nu, b0)
        tab[2, n] = upper(nu, b0)
        tab[3, n] = slot_node(n, b2)
        tab[4, n] = node_slot(lower(n, b3), b2)
        tab[5, n] = node_slot(upper(n, b3), b2)

    def remote(source, target, send, recv, peer):
        return pltpu.make_async_remote_copy(
            src_ref=source, dst_ref=target, send_sem=send, recv_sem=recv, device_id=peer, device_id_type=MESH
        )

    def copy1(c, s):
        return remote(s0.at[c, s], r1.at[c, s], send1.at[c, s], recv1.at[c, s], peer1)

    def copy3(c, s):
        return remote(s2.at[c, s], r3.at[c, s], send3.at[c, s], recv3.at[c, s], peer3)

    def copym(c, i):
        q = flip(near, i)
        return remote(
            pm.at[c, :, q], mid.at[c, :, near], sendm.at[c, i], recvm.at[c, i], (src, flip(tgt, i))
        )

    def copy4(c, k):
        return remote(t4.at[c, k], s4.at[c, HALF * far + spot[k]], send4.at[c, k], recv4.at[c, k], peer4)

    def copy6(c, s):
        return remote(s5.at[c, s], r6.at[c, s], send6.at[c, s], recv6.at[c, s], peer6)

    def copyg():
        return remote(g_hbm.at[4, pl.ds(HALF * (1 - far), HALF)], gpart, gs_sem, gr_sem, peer4)

    def copyo(c):
        return pltpu.make_async_copy(
            out.at[c], out_hbm.at[:, :, pl.ds(pl.multiple_of(c * WIDTH, WIDTH), WIDTH)], out_sem.at[c]
        )

    def convert(level, slot, first, second):
        for half, block in ((0, first), (1, second)):
            high = block.astype(BF16)
            gb[level, slot, :RANK, half * RANK : (half + 1) * RANK] = high
            gb[level, slot, RANK:, half * RANK : (half + 1) * RANK] = (block - high.astype(F32)).astype(BF16)

    load_g0.wait()
    for s in range(NODES):
        block = graw0[tab[0, s]]
        convert(0, s, block[:, :RANK], block[:, RANK:])
    load_g.start()
    pl.semaphore_wait(barrier, len(peers))
    copyg().start()

    def phase_a(c, carry):
        copyx(c).wait()
        for n in range(NODES):
            xa[n] = split(x0[c, n])
        for group in ((0, 1), (2, 3, 4), (5, 6, 7)):
            for s in group:
                (s0[c, s],) = product(gb[0, s], stack(xa[tab[1, s]], xa[tab[2, s]]))
            for s in group:
                copy1(c, s).start()
        return carry

    lax.fori_loop(0, CHUNKS, phase_a, 0)

    load_g.wait()

    def convert_slot(s, carry):
        for level, row in ((2, 0), (5, 3)):
            block = graw[level - 1, tab[row, s]]
            convert(level, s, block[:, :RANK], block[:, RANK:])
        block = graw[6, s]
        convert(7, s, block[:, :RANK], block[:, RANK:])
        for level, row, side in ((1, 0, side1), (3, 0, side3), (6, 3, side6)):
            first = graw[level - 1, tab[row, s], :, pl.ds(pl.multiple_of(side * RANK, RANK), RANK)]
            second = graw[level - 1, tab[row, s], :, pl.ds(pl.multiple_of((1 - side) * RANK, RANK), RANK)]
            convert(level, s, first, second)
        return carry

    lax.fori_loop(0, NODES, convert_slot, 0)

    rows = relabel[...]
    node, row = rows >> 7, rows & 127
    position = (node_slot(node, b1) * RANK + row).astype(F32)
    lanes = lax.broadcasted_iota(jnp.int32, (RANK, RANK), 1).astype(F32)
    for q in range(NODES):
        wanted = jnp.broadcast_to(position[q : q + 1, :], (RANK, RANK)).T
        for k in range(NODES):
            onehot[q * RANK : (q + 1) * RANK, k * RANK : (k + 1) * RANK] = jnp.where(
                wanted == lanes + float(k * RANK), 1.0, 0.0
            ).astype(BF16)

    copyg().wait_recv()
    for k in range(HALF):
        block = graw[3, HALF * far + spot[k]]
        convert(4, 2 * k, block[:, :RANK], block[:, RANK:])
        block = gpart[spot[k]]
        convert(4, 2 * k + 1, block[:, :RANK], block[:, RANK:])

    def phase_b(c):
        for i in range(HALF):
            parts = []
            for s in (2 * i, 2 * i + 1):
                copy1(c, s).wait_recv()
            for s in (2 * i, 2 * i + 1):
                (y,) = product(gb[1, s], stack(split(s0[c, s]), split(r1[c, s])))
                parts.append(split(y))
            ys = product(gb[2, 2 * i : 2 * i + 2].reshape(4 * RANK, 2 * RANK), stack(*parts))
            for s, y in zip((2 * i, 2 * i + 1), ys):
                s2[c, s] = y
            for s in (2 * i, 2 * i + 1):
                copy3(c, s).start()

    def phase_c(c):
        for group in ((0, 1, 2, 3), (4, 5, 6, 7)):
            for s in group:
                copy3(c, s).wait_recv()
            for s in group:
                (y,) = product(gb[3, s], stack(split(s2[c, s]), split(r3[c, s])))
                xc[s * RANK : (s + 1) * RANK, :] = split(y)
        state = xc[...]
        for q in range(4):
            full = jnp.dot(onehot[q * 256 : (q + 1) * 256, :], state, preferred_element_type=F32)
            picked = full[:, :WIDTH] + full[:, WIDTH:]
            for k in range(4):
                t = 4 * q + k
                pm[c, t // 8, t % 8] = picked[k * 64 : (k + 1) * 64]
        for i in (6, 7, 4, 5, 2, 3, 1):
            copym(c, i).start()
        mid[c, 0, near] = pm[c, 0, near]
        mid[c, 1, near] = pm[c, 1, near]

    def phase_d(c, order):
        for k in order:
            for i in (2 * k, 2 * k + 1):
                if i:
                    copym(c, i).wait_recv()
        for k in order:
            parts = [split(mid[c, e, pl.ds(2 * spot[k], 2)].reshape(RANK, WIDTH)) for e in range(2)]
            own, other = product(gb[4, 2 * k : 2 * k + 2].reshape(4 * RANK, 2 * RANK), stack(*parts))
            t4[c, k] = other
            s4[c, HALF * far + spot[k]] = own
        for k in order:
            copy4(c, k).start()

    def phase_e(c):
        for n in range(HALF):
            copy4(c, n).wait_recv()
        for n in range(NODES):
            xe[n] = split(s4[c, n])
        for i in range(HALF):
            state = stack(xe[tab[3, 2 * i]], xe[tab[3, 2 * i + 1]])
            ys = product(gb[5, 2 * i : 2 * i + 2].reshape(4 * RANK, 2 * RANK), state)
            for s, y in zip((2 * i, 2 * i + 1), ys):
                s5[c, s] = y
        for s in range(NODES):
            copy6(c, s).start()

    def phase_f(c):
        for s in range(NODES):
            copy6(c, s).wait_recv()
        for s in range(NODES):
            (y,) = product(gb[6, s], stack(split(s5[c, s]), split(r6[c, s])))
            xf[s] = split(y)
        for n in range(NODES):
            (y,) = product(gb[7, n], stack(xf[tab[4, n]], xf[tab[5, n]]))
            out[c, n] = y
        copyo(c).start()

    def step(k, carry):
        for delay, phase in (
            (1, phase_c),
            (0, phase_b),
            (4, functools.partial(phase_d, order=(3, 1))),
            (2, functools.partial(phase_d, order=(0, 2))),
            (5, phase_e),
            (6, phase_f),
        ):

            @pl.when(jnp.logical_and(k >= delay, k < delay + CHUNKS))
            def _(delay=delay, phase=phase):
                phase(k - delay)

        return carry

    lax.fori_loop(0, CHUNKS + 6, step, 0)

    copyg().wait_send()

    def finish(c, carry):
        for s in range(NODES):
            copy1(c, s).wait_send()
            copy3(c, s).wait_send()
            copy6(c, s).wait_send()
        for i in range(1, 8):
            copym(c, i).wait_send()
        for n in range(HALF):
            copy4(c, n).wait_send()
        copyo(c).wait()
        return carry

    lax.fori_loop(0, CHUNKS, finish, 0)


def on_device(coefficients, transfer, local_bits, relabel):
    state = (CHUNKS, NODES, RANK, WIDTH)
    halves = (CHUNKS, 2, 8, 64, WIDTH)
    dma = pltpu.SemaphoreType.DMA
    return pl.pallas_call(
        kernel,
        out_shape=jax.ShapeDtypeStruct(coefficients.shape, F32),
        in_specs=[
            pl.BlockSpec(memory_space=pltpu.SMEM),
            pl.BlockSpec(memory_space=pltpu.VMEM),
            pl.BlockSpec(memory_space=pltpu.HBM),
            pl.BlockSpec(memory_space=pltpu.HBM),
        ],
        out_specs=pl.BlockSpec(memory_space=pl.ANY),
        scratch_shapes=[
            pltpu.VMEM(state, F32),
            pltpu.VMEM((NODES, RANK, 2 * RANK), F32),
            pltpu.VMEM((7, NODES, RANK, 2 * RANK), F32),
            pltpu.VMEM((HALF, RANK, 2 * RANK), F32),
            pltpu.VMEM((8, NODES, 2 * RANK, 2 * RANK), BF16),
            pltpu.VMEM((NODES, RANK, 2 * WIDTH), BF16),
            pltpu.VMEM((NODES * RANK, 2 * WIDTH), BF16),
            pltpu.VMEM((NODES, RANK, 2 * WIDTH), BF16),
            pltpu.VMEM((NODES, RANK, 2 * WIDTH), BF16),
            pltpu.VMEM((NODES * RANK, NODES * RANK), BF16),
            pltpu.VMEM(state, F32),
            pltpu.VMEM(state, F32),
            pltpu.VMEM(state, F32),
            pltpu.VMEM(state, F32),
            pltpu.VMEM(halves, F32),
            pltpu.VMEM(halves, F32),
            pltpu.VMEM((CHUNKS, HALF, RANK, WIDTH), F32),
            pltpu.VMEM(state, F32),
            pltpu.VMEM(state, F32),
            pltpu.VMEM(state, F32),
            pltpu.VMEM(state, F32),
            pltpu.SMEM((6, NODES), jnp.int32),
            dma((2,)),
            dma((CHUNKS,)),
            dma,
            dma,
            dma((CHUNKS, NODES)),
            dma((CHUNKS, NODES)),
            dma((CHUNKS, NODES)),
            dma((CHUNKS, NODES)),
            dma((CHUNKS, NODES)),
            dma((CHUNKS, NODES)),
            dma((CHUNKS, HALF)),
            dma((CHUNKS, HALF)),
            dma((CHUNKS, NODES)),
            dma((CHUNKS, NODES)),
            dma((CHUNKS,)),
        ],
        compiler_params=pltpu.CompilerParams(
            collective_id=1, has_side_effects=True, vmem_limit_bytes=50 * 2**20
        ),
    )(local_bits, relabel.reshape(8, 128), coefficients, transfer)


def solution(mesh):
    placed = (P(("src", "tgt"), None, None), P(None, ("src", "tgt"), None, None), P(), P())
    return jax.shard_map(
        on_device,
        mesh=mesh,
        in_specs=placed,
        out_specs=P(("src", "tgt"), None, None),
        check_vma=False,
    )
```

```python
import functools

import jax
import jax.numpy as jnp
from jax import lax
from jax.experimental import pallas as pl
from jax.experimental.pallas import tpu as pltpu
from jax.sharding import PartitionSpec as P

MESH = pl.DeviceIdType.MESH
F32 = jnp.float32
BF16 = jnp.bfloat16
CHUNKS = 4
WIDTH = 128
RANK = 128
NODES = 8
HALF = 4


def flip(index, mask):
    for bit in (1, 2, 4, 8):
        if mask & bit:
            index = index + bit - 2 * bit * (lax.div(index, bit) % 2)
    return index


def pick(bit, options):
    return jnp.where(bit == 0, options[0], jnp.where(bit == 1, options[1], options[2]))


def bits_of(number):
    return (number >> 2) & 1, (number >> 1) & 1, number & 1


def slot_node(slot, bit):
    a, b, e = bits_of(slot)
    return pick(bit, (4 * a + 2 * b + e, 4 * a + 2 * e + b, 4 * e + 2 * a + b))


def node_slot(node, bit):
    c, b, a = bits_of(node)
    return pick(bit, (4 * c + 2 * b + a, 4 * c + 2 * a + b, 4 * b + 2 * a + c))


def lower(node, bit):
    return pick(bit, (node & ~1, node & ~2, node & ~4))


def upper(node, bit):
    return pick(bit, (node | 1, node | 2, node | 4))


def split(value):
    high = value.astype(BF16)
    low = (value - high.astype(F32)).astype(BF16)
    return jnp.concatenate([high, low], axis=1)


def product(block, state):
    full = jnp.dot(block, state, preferred_element_type=F32)
    both = full[:, :WIDTH] + full[:, WIDTH:]
    return [both[r : r + RANK] + both[r + RANK : r + 2 * RANK] for r in range(0, both.shape[0], 2 * RANK)]


def stack(first, second):
    return jnp.concatenate([first, second], axis=0)


def kernel(
    bits, relabel, coef_hbm, g_hbm, out_hbm,
    x0, graw0, graw, gpart, gb, xa, xc, xe, xf, onehot,
    s0, r1, s2, r3, pm, mid, t4, s4, s5, r6, out,
    tab, in_sem, x_sem, gs_sem, gr_sem,
    send1, recv1, send3, recv3, sendm, recvm, send4, recv4, send6, recv6, out_sem,
):
    src = lax.axis_index("src")
    tgt = lax.axis_index("tgt")
    far = lax.div(tgt, 8)
    near = tgt % 8
    spot = [flip(lax.div(near, 2), k) for k in range(HALF)]
    peer1 = (flip(src, 8), tgt)
    peer3 = (flip(src, 1), tgt)
    peer4 = (src, flip(tgt, 8))
    peer6 = (src, flip(tgt, 1))
    side1 = lax.div(src, 8)
    side3 = src % 2
    side6 = tgt % 2

    barrier = pltpu.get_barrier_semaphore()
    peers = [peer1, peer3, peer4] + [(src, flip(tgt, i)) for i in range(1, 8)]
    for peer in peers:
        pl.semaphore_signal(barrier, inc=1, device_id=peer, device_id_type=MESH)

    def copyx(c):
        columns = pl.ds(pl.multiple_of(c * WIDTH, WIDTH), WIDTH)
        return pltpu.make_async_copy(coef_hbm.at[:, :, columns], x0.at[c], x_sem.at[c])

    load_g0 = pltpu.make_async_copy(g_hbm.at[0], graw0, in_sem.at[0])
    load_g = pltpu.make_async_copy(g_hbm.at[pl.ds(1, 7)], graw, in_sem.at[1])
    load_g0.start()
    for c in range(CHUNKS):
        copyx(c).start()

    b0, b1, b2, b3 = bits[0], bits[1], bits[2], bits[3]
    for n in range(NODES):
        nu = slot_node(n, b1)
        tab[0, n] = nu
        tab[1, n] = lower(nu, b0)
        tab[2, n] = upper(nu, b0)
        tab[3, n] = slot_node(n, b2)
        tab[4, n] = node_slot(lower(n, b3), b2)
        tab[5, n] = node_slot(upper(n, b3), b2)

    def remote(source, target, send, recv, peer):
        return pltpu.make_async_remote_copy(
            src_ref=source, dst_ref=target, send_sem=send, recv_sem=recv, device_id=peer, device_id_type=MESH
        )

    def copy1(c, s):
        return remote(s0.at[c, s], r1.at[c, s], send1.at[c, s], recv1.at[c, s], peer1)

    def copy3(c, s):
        return remote(s2.at[c, s], r3.at[c, s], send3.at[c, s], recv3.at[c, s], peer3)

    def copym(c, i):
        q = flip(near, i)
        return remote(
            pm.at[c, :, q], mid.at[c, :, near], sendm.at[c, i], recvm.at[c, i], (src, flip(tgt, i))
        )

    def copy4(c, k):
        return remote(t4.at[c, k], s4.at[c, HALF * far + spot[k]], send4.at[c, k], recv4.at[c, k], peer4)

    def copy6(c, s):
        return remote(s5.at[c, s], r6.at[c, s], send6.at[c, s], recv6.at[c, s], peer6)

    def copyg():
        return remote(g_hbm.at[4, pl.ds(HALF * (1 - far), HALF)], gpart, gs_sem, gr_sem, peer4)

    def copyo(c):
        return pltpu.make_async_copy(
            out.at[c], out_hbm.at[:, :, pl.ds(pl.multiple_of(c * WIDTH, WIDTH), WIDTH)], out_sem.at[c]
        )

    def convert(level, slot, first, second):
        for half, block in ((0, first), (1, second)):
            high = block.astype(BF16)
            gb[level, slot, :RANK, half * RANK : (half + 1) * RANK] = high
            gb[level, slot, RANK:, half * RANK : (half + 1) * RANK] = (block - high.astype(F32)).astype(BF16)

    load_g0.wait()
    for s in range(NODES):
        block = graw0[tab[0, s]]
        convert(0, s, block[:, :RANK], block[:, RANK:])
    load_g.start()
    pl.semaphore_wait(barrier, len(peers))
    copyg().start()

    def phase_a(c, carry):
        copyx(c).wait()
        for n in range(NODES):
            xa[n] = split(x0[c, n])
        for group in ((0, 1), (2, 3, 4), (5, 6, 7)):
            for s in group:
                (s0[c, s],) = product(gb[0, s], stack(xa[tab[1, s]], xa[tab[2, s]]))
            for s in group:
                copy1(c, s).start()
        return carry

    lax.fori_loop(0, CHUNKS, phase_a, 0)

    load_g.wait()

    def convert_slot(s, carry):
        for level, row in ((2, 0), (5, 3)):
            block = graw[level - 1, tab[row, s]]
            convert(level, s, block[:, :RANK], block[:, RANK:])
        block = graw[6, s]
        convert(7, s, block[:, :RANK], block[:, RANK:])
        for level, row, side in ((1, 0, side1), (3, 0, side3), (6, 3, side6)):
            first = graw[level - 1, tab[row, s], :, pl.ds(pl.multiple_of(side * RANK, RANK), RANK)]
            second = graw[level - 1, tab[row, s], :, pl.ds(pl.multiple_of((1 - side) * RANK, RANK), RANK)]
            convert(level, s, first, second)
        return carry

    lax.fori_loop(0, NODES, convert_slot, 0)

    rows = relabel[...]
    node, row = rows >> 7, rows & 127
    position = (node_slot(node, b1) * RANK + row).astype(F32)
    lanes = lax.broadcasted_iota(jnp.int32, (RANK, RANK), 1).astype(F32)
    for q in range(NODES):
        wanted = jnp.broadcast_to(position[q : q + 1, :], (RANK, RANK)).T
        for k in range(NODES):
            onehot[q * RANK : (q + 1) * RANK, k * RANK : (k + 1) * RANK] = jnp.where(
                wanted == lanes + float(k * RANK), 1.0, 0.0
            ).astype(BF16)

    copyg().wait_recv()
    for k in range(HALF):
        block = graw[3, HALF * far + spot[k]]
        convert(4, 2 * k, block[:, :RANK], block[:, RANK:])
        block = gpart[spot[k]]
        convert(4, 2 * k + 1, block[:, :RANK], block[:, RANK:])

    def phase_b(c, pairs):
        for i in pairs:
            parts = []
            for s in (2 * i, 2 * i + 1):
                copy1(c, s).wait_recv()
            for s in (2 * i, 2 * i + 1):
                (y,) = product(gb[1, s], stack(split(s0[c, s]), split(r1[c, s])))
                parts.append(split(y))
            ys = product(gb[2, 2 * i : 2 * i + 2].reshape(4 * RANK, 2 * RANK), stack(*parts))
            for s, y in zip((2 * i, 2 * i + 1), ys):
                s2[c, s] = y
            for s in (2 * i, 2 * i + 1):
                copy3(c, s).start()

    def phase_c(c):
        for group in ((0, 1, 2, 3), (4, 5, 6, 7)):
            for s in group:
                copy3(c, s).wait_recv()
            for s in group:
                (y,) = product(gb[3, s], stack(split(s2[c, s]), split(r3[c, s])))
                xc[s * RANK : (s + 1) * RANK, :] = split(y)
        state = xc[...]
        for q in range(4):
            full = jnp.dot(onehot[q * 256 : (q + 1) * 256, :], state, preferred_element_type=F32)
            picked = full[:, :WIDTH] + full[:, WIDTH:]
            for k in range(4):
                t = 4 * q + k
                pm[c, t // 8, t % 8] = picked[k * 64 : (k + 1) * 64]
        for i in (4, 5, 6, 7, 2, 3, 1):
            copym(c, i).start()
        mid[c, 0, near] = pm[c, 0, near]
        mid[c, 1, near] = pm[c, 1, near]

    def phase_d(c, order):
        for k in order:
            for i in (2 * k, 2 * k + 1):
                if i:
                    copym(c, i).wait_recv()
        for k in order:
            parts = [split(mid[c, e, pl.ds(2 * spot[k], 2)].reshape(RANK, WIDTH)) for e in range(2)]
            own, other = product(gb[4, 2 * k : 2 * k + 2].reshape(4 * RANK, 2 * RANK), stack(*parts))
            t4[c, k] = other
            s4[c, HALF * far + spot[k]] = own
        for k in order:
            copy4(c, k).start()

    def phase_e(c):
        for n in range(HALF):
            copy4(c, n).wait_recv()
        for n in range(NODES):
            xe[n] = split(s4[c, n])
        for i in range(HALF):
            state = stack(xe[tab[3, 2 * i]], xe[tab[3, 2 * i + 1]])
            ys = product(gb[5, 2 * i : 2 * i + 2].reshape(4 * RANK, 2 * RANK), state)
            for s, y in zip((2 * i, 2 * i + 1), ys):
                s5[c, s] = y
        for s in range(NODES):
            copy6(c, s).start()

    def phase_f(c):
        for s in range(NODES):
            copy6(c, s).wait_recv()
        for s in range(NODES):
            (y,) = product(gb[6, s], stack(split(s5[c, s]), split(r6[c, s])))
            xf[s] = split(y)
        for n in range(NODES):
            (y,) = product(gb[7, n], stack(xf[tab[4, n]], xf[tab[5, n]]))
            out[c, n] = y
        copyo(c).start()

    def step(k, carry):
        early = functools.partial(phase_d, order=(0, 2))
        late = functools.partial(phase_d, order=(3, 1))
        for delay, first, last, phase in (
            (1, 0, 3, phase_c),
            (2, 0, 1, early),
            (0, 0, 3, functools.partial(phase_b, pairs=(0, 1))),
            (1, 2, 2, early),
            (0, 0, 3, functools.partial(phase_b, pairs=(2, 3))),
            (4, 0, 3, late),
            (2, 3, 3, early),
            (5, 0, 3, phase_e),
            (6, 0, 3, phase_f),
        ):

            @pl.when(jnp.logical_and(k >= delay + first, k <= delay + last))
            def _(delay=delay, phase=phase):
                phase(k - delay)

        return carry

    lax.fori_loop(0, CHUNKS + 6, step, 0)

    copyg().wait_send()

    def finish(c, carry):
        for s in range(NODES):
            copy1(c, s).wait_send()
            copy3(c, s).wait_send()
            copy6(c, s).wait_send()
        for i in range(1, 8):
            copym(c, i).wait_send()
        for n in range(HALF):
            copy4(c, n).wait_send()
        copyo(c).wait()
        return carry

    lax.fori_loop(0, CHUNKS, finish, 0)


def on_device(coefficients, transfer, local_bits, relabel):
    state = (CHUNKS, NODES, RANK, WIDTH)
    halves = (CHUNKS, 2, 8, 64, WIDTH)
    dma = pltpu.SemaphoreType.DMA
    return pl.pallas_call(
        kernel,
        out_shape=jax.ShapeDtypeStruct(coefficients.shape, F32),
        in_specs=[
            pl.BlockSpec(memory_space=pltpu.SMEM),
            pl.BlockSpec(memory_space=pltpu.VMEM),
            pl.BlockSpec(memory_space=pltpu.HBM),
            pl.BlockSpec(memory_space=pltpu.HBM),
        ],
        out_specs=pl.BlockSpec(memory_space=pl.ANY),
        scratch_shapes=[
            pltpu.VMEM(state, F32),
            pltpu.VMEM((NODES, RANK, 2 * RANK), F32),
            pltpu.VMEM((7, NODES, RANK, 2 * RANK), F32),
            pltpu.VMEM((HALF, RANK, 2 * RANK), F32),
            pltpu.VMEM((8, NODES, 2 * RANK, 2 * RANK), BF16),
            pltpu.VMEM((NODES, RANK, 2 * WIDTH), BF16),
            pltpu.VMEM((NODES * RANK, 2 * WIDTH), BF16),
            pltpu.VMEM((NODES, RANK, 2 * WIDTH), BF16),
            pltpu.VMEM((NODES, RANK, 2 * WIDTH), BF16),
            pltpu.VMEM((NODES * RANK, NODES * RANK), BF16),
            pltpu.VMEM(state, F32),
            pltpu.VMEM(state, F32),
            pltpu.VMEM(state, F32),
            pltpu.VMEM(state, F32),
            pltpu.VMEM(halves, F32),
            pltpu.VMEM(halves, F32),
            pltpu.VMEM((CHUNKS, HALF, RANK, WIDTH), F32),
            pltpu.VMEM(state, F32),
            pltpu.VMEM(state, F32),
            pltpu.VMEM(state, F32),
            pltpu.VMEM(state, F32),
            pltpu.SMEM((6, NODES), jnp.int32),
            dma((2,)),
            dma((CHUNKS,)),
            dma,
            dma,
            dma((CHUNKS, NODES)),
            dma((CHUNKS, NODES)),
            dma((CHUNKS, NODES)),
            dma((CHUNKS, NODES)),
            dma((CHUNKS, NODES)),
            dma((CHUNKS, NODES)),
            dma((CHUNKS, HALF)),
            dma((CHUNKS, HALF)),
            dma((CHUNKS, NODES)),
            dma((CHUNKS, NODES)),
            dma((CHUNKS,)),
        ],
        compiler_params=pltpu.CompilerParams(
            collective_id=1, has_side_effects=True, vmem_limit_bytes=50 * 2**20
        ),
    )(local_bits, relabel.reshape(8, 128), coefficients, transfer)


def solution(mesh):
    placed = (P(("src", "tgt"), None, None), P(None, ("src", "tgt"), None, None), P(), P())
    return jax.shard_map(
        on_device,
        mesh=mesh,
        in_specs=placed,
        out_specs=P(("src", "tgt"), None, None),
        check_vma=False,
    )
```

```python
import functools

import jax
import jax.numpy as jnp
from jax import lax
from jax.experimental import pallas as pl
from jax.experimental.pallas import tpu as pltpu
from jax.sharding import PartitionSpec as P

MESH = pl.DeviceIdType.MESH
F32 = jnp.float32
BF16 = jnp.bfloat16
CHUNKS = 4
WIDTH = 128
RANK = 128
NODES = 8
HALF = 4


def flip(index, mask):
    for bit in (1, 2, 4, 8):
        if mask & bit:
            index = index + bit - 2 * bit * (lax.div(index, bit) % 2)
    return index


def pick(bit, options):
    return jnp.where(bit == 0, options[0], jnp.where(bit == 1, options[1], options[2]))


def bits_of(number):
    return (number >> 2) & 1, (number >> 1) & 1, number & 1


def slot_node(slot, bit):
    a, b, e = bits_of(slot)
    return pick(bit, (4 * a + 2 * b + e, 4 * a + 2 * e + b, 4 * e + 2 * a + b))


def node_slot(node, bit):
    c, b, a = bits_of(node)
    return pick(bit, (4 * c + 2 * b + a, 4 * c + 2 * a + b, 4 * b + 2 * a + c))


def lower(node, bit):
    return pick(bit, (node & ~1, node & ~2, node & ~4))


def upper(node, bit):
    return pick(bit, (node | 1, node | 2, node | 4))


def split(value):
    high = value.astype(BF16)
    low = (value - high.astype(F32)).astype(BF16)
    return jnp.concatenate([high, low], axis=1)


def product(block, state):
    full = jnp.dot(block, state, preferred_element_type=F32)
    both = full[:, :WIDTH] + full[:, WIDTH:]
    return [both[r : r + RANK] + both[r + RANK : r + 2 * RANK] for r in range(0, both.shape[0], 2 * RANK)]


def stack(first, second):
    return jnp.concatenate([first, second], axis=0)


def kernel(
    bits, relabel, coef_hbm, g_hbm, out_hbm,
    x0, graw0, graw, gpart, gb, xa, xc, xe, xf, onehot,
    s0, r1, s2, r3, pm, mid, t4, s4, s5, r6, out,
    tab, in_sem, x_sem, gs_sem, gr_sem,
    send1, recv1, send3, recv3, sendm, recvm, send4, recv4, send6, recv6, out_sem,
):
    src = lax.axis_index("src")
    tgt = lax.axis_index("tgt")
    far = lax.div(tgt, 8)
    near = tgt % 8
    spot = [flip(lax.div(near, 2), k) for k in range(HALF)]
    peer1 = (flip(src, 8), tgt)
    peer3 = (flip(src, 1), tgt)
    peer4 = (src, flip(tgt, 8))
    peer6 = (src, flip(tgt, 1))
    side1 = lax.div(src, 8)
    side3 = src % 2
    side6 = tgt % 2

    barrier = pltpu.get_barrier_semaphore()
    peers = [peer1, peer3, peer4] + [(src, flip(tgt, i)) for i in range(1, 8)]
    for peer in peers:
        pl.semaphore_signal(barrier, inc=1, device_id=peer, device_id_type=MESH)

    def copyx(c):
        columns = pl.ds(pl.multiple_of(c * WIDTH, WIDTH), WIDTH)
        return pltpu.make_async_copy(coef_hbm.at[:, :, columns], x0.at[c], x_sem.at[c])

    load_g0 = pltpu.make_async_copy(g_hbm.at[0], graw0, in_sem.at[0])
    load_g = pltpu.make_async_copy(g_hbm.at[pl.ds(1, 7)], graw, in_sem.at[1])
    load_g0.start()
    for c in range(CHUNKS):
        copyx(c).start()

    b0, b1, b2, b3 = bits[0], bits[1], bits[2], bits[3]
    for n in range(NODES):
        nu = slot_node(n, b1)
        tab[0, n] = nu
        tab[1, n] = lower(nu, b0)
        tab[2, n] = upper(nu, b0)
        tab[3, n] = slot_node(n, b2)
        tab[4, n] = node_slot(lower(n, b3), b2)
        tab[5, n] = node_slot(upper(n, b3), b2)

    def remote(source, target, send, recv, peer):
        return pltpu.make_async_remote_copy(
            src_ref=source, dst_ref=target, send_sem=send, recv_sem=recv, device_id=peer, device_id_type=MESH
        )

    def copy1(c, s):
        return remote(s0.at[c, s], r1.at[c, s], send1.at[c, s], recv1.at[c, s], peer1)

    def copy3(c, s):
        return remote(s2.at[c, s], r3.at[c, s], send3.at[c, s], recv3.at[c, s], peer3)

    def copym(c, i):
        q = flip(near, i)
        return remote(
            pm.at[c, :, q], mid.at[c, :, near], sendm.at[c, i], recvm.at[c, i], (src, flip(tgt, i))
        )

    def copy4(c, k):
        return remote(t4.at[c, k], s4.at[c, HALF * far + spot[k]], send4.at[c, k], recv4.at[c, k], peer4)

    def copy6(c, s):
        return remote(s5.at[c, s], r6.at[c, s], send6.at[c, s], recv6.at[c, s], peer6)

    def copyg():
        return remote(g_hbm.at[4, pl.ds(HALF * (1 - far), HALF)], gpart, gs_sem, gr_sem, peer4)

    def copyo(c, h):
        columns = pl.ds(pl.multiple_of(c * WIDTH, WIDTH), WIDTH)
        nodes = pl.ds(h * HALF, HALF)
        return pltpu.make_async_copy(out.at[c, nodes], out_hbm.at[nodes, :, columns], out_sem.at[c, h])

    def convert(level, slot, first, second):
        for half, block in ((0, first), (1, second)):
            high = block.astype(BF16)
            gb[level, slot, :RANK, half * RANK : (half + 1) * RANK] = high
            gb[level, slot, RANK:, half * RANK : (half + 1) * RANK] = (block - high.astype(F32)).astype(BF16)

    load_g0.wait()
    for s in range(NODES):
        block = graw0[tab[0, s]]
        convert(0, s, block[:, :RANK], block[:, RANK:])
    load_g.start()

    def phase_a(c, carry):
        copyx(c).wait()
        for n in range(NODES):
            xa[n] = split(x0[c, n])
        for group in ((0, 1), (2, 3, 4), (5, 6, 7)):
            for s in group:
                (s0[c, s],) = product(gb[0, s], stack(xa[tab[1, s]], xa[tab[2, s]]))
            if group[0] == 0:

                @pl.when(c == 0)
                def _():
                    pl.semaphore_wait(barrier, len(peers))
                    copyg().start()

            for s in group:
                copy1(c, s).start()
        return carry

    lax.fori_loop(0, CHUNKS, phase_a, 0)

    load_g.wait()

    def convert_slot(s, carry):
        for level, row in ((2, 0), (5, 3)):
            block = graw[level - 1, tab[row, s]]
            convert(level, s, block[:, :RANK], block[:, RANK:])
        block = graw[6, s]
        convert(7, s, block[:, :RANK], block[:, RANK:])
        for level, row, side in ((1, 0, side1), (3, 0, side3), (6, 3, side6)):
            first = graw[level - 1, tab[row, s], :, pl.ds(pl.multiple_of(side * RANK, RANK), RANK)]
            second = graw[level - 1, tab[row, s], :, pl.ds(pl.multiple_of((1 - side) * RANK, RANK), RANK)]
            convert(level, s, first, second)
        return carry

    lax.fori_loop(0, NODES, convert_slot, 0)

    rows = relabel[...]
    node, row = rows >> 7, rows & 127
    position = (node_slot(node, b1) * RANK + row).astype(F32)
    lanes = lax.broadcasted_iota(jnp.int32, (RANK, RANK), 1).astype(F32)
    for q in range(NODES):
        wanted = jnp.broadcast_to(position[q : q + 1, :], (RANK, RANK)).T
        for k in range(NODES):
            onehot[q * RANK : (q + 1) * RANK, k * RANK : (k + 1) * RANK] = jnp.where(
                wanted == lanes + float(k * RANK), 1.0, 0.0
            ).astype(BF16)

    copyg().wait_recv()
    for k in range(HALF):
        block = graw[3, HALF * far + spot[k]]
        convert(4, 2 * k, block[:, :RANK], block[:, RANK:])
        block = gpart[spot[k]]
        convert(4, 2 * k + 1, block[:, :RANK], block[:, RANK:])

    def phase_b(c, pairs):
        for i in pairs:
            parts = []
            for s in (2 * i, 2 * i + 1):
                copy1(c, s).wait_recv()
            for s in (2 * i, 2 * i + 1):
                (y,) = product(gb[1, s], stack(split(s0[c, s]), split(r1[c, s])))
                parts.append(split(y))
            ys = product(gb[2, 2 * i : 2 * i + 2].reshape(4 * RANK, 2 * RANK), stack(*parts))
            for s, y in zip((2 * i, 2 * i + 1), ys):
                s2[c, s] = y
            for s in (2 * i, 2 * i + 1):
                copy3(c, s).start()

    def phase_c(c):
        for group in ((0, 1, 2, 3), (4, 5, 6, 7)):
            for s in group:
                copy3(c, s).wait_recv()
            for s in group:
                (y,) = product(gb[3, s], stack(split(s2[c, s]), split(r3[c, s])))
                xc[s * RANK : (s + 1) * RANK, :] = split(y)
        state = xc[...]
        for q in range(4):
            full = jnp.dot(onehot[q * 256 : (q + 1) * 256, :], state, preferred_element_type=F32)
            picked = full[:, :WIDTH] + full[:, WIDTH:]
            for k in range(4):
                t = 4 * q + k
                pm[c, t // 8, t % 8] = picked[k * 64 : (k + 1) * 64]
        for i in (4, 5, 6, 7, 2, 3, 1):
            copym(c, i).start()
        mid[c, 0, near] = pm[c, 0, near]
        mid[c, 1, near] = pm[c, 1, near]

    def phase_d(c, order):
        for k in order:
            for i in (2 * k, 2 * k + 1):
                if i:
                    copym(c, i).wait_recv()
        for k in order:
            parts = [split(mid[c, e, pl.ds(2 * spot[k], 2)].reshape(RANK, WIDTH)) for e in range(2)]
            own, other = product(gb[4, 2 * k : 2 * k + 2].reshape(4 * RANK, 2 * RANK), stack(*parts))
            t4[c, k] = other
            s4[c, HALF * far + spot[k]] = own
        for k in order:
            copy4(c, k).start()

    def phase_e(c):
        for n in range(HALF):
            copy4(c, n).wait_recv()
        for n in range(NODES):
            xe[n] = split(s4[c, n])
        for i in range(HALF):
            state = stack(xe[tab[3, 2 * i]], xe[tab[3, 2 * i + 1]])
            ys = product(gb[5, 2 * i : 2 * i + 2].reshape(4 * RANK, 2 * RANK), state)
            for s, y in zip((2 * i, 2 * i + 1), ys):
                s5[c, s] = y
        for s in range(NODES):
            copy6(c, s).start()

    def phase_f(c):
        for s in range(NODES):
            copy6(c, s).wait_recv()
        for s in range(NODES):
            (y,) = product(gb[6, s], stack(split(s5[c, s]), split(r6[c, s])))
            xf[s] = split(y)
        for n in range(NODES):
            (y,) = product(gb[7, n], stack(xf[tab[4, n]], xf[tab[5, n]]))
            out[c, n] = y
            if n % HALF == HALF - 1:
                copyo(c, n // HALF).start()

    def step(k, carry):
        early = functools.partial(phase_d, order=(0, 2))
        late = functools.partial(phase_d, order=(3, 1))
        for delay, first, last, phase in (
            (1, 0, 3, phase_c),
            (2, 0, 1, early),
            (0, 0, 3, functools.partial(phase_b, pairs=(0, 1))),
            (1, 2, 2, early),
            (0, 0, 3, functools.partial(phase_b, pairs=(2, 3))),
            (4, 0, 3, late),
            (2, 3, 3, early),
            (5, 0, 3, phase_e),
            (6, 0, 3, phase_f),
        ):

            @pl.when(jnp.logical_and(k >= delay + first, k <= delay + last))
            def _(delay=delay, phase=phase):
                phase(k - delay)

        return carry

    lax.fori_loop(0, CHUNKS + 6, step, 0)

    copyg().wait_send()

    def finish(c, carry):
        for s in range(NODES):
            copy1(c, s).wait_send()
            copy3(c, s).wait_send()
            copy6(c, s).wait_send()
        for i in range(1, 8):
            copym(c, i).wait_send()
        for n in range(HALF):
            copy4(c, n).wait_send()
        for h in range(2):
            copyo(c, h).wait()
        return carry

    lax.fori_loop(0, CHUNKS, finish, 0)


def on_device(coefficients, transfer, local_bits, relabel):
    state = (CHUNKS, NODES, RANK, WIDTH)
    halves = (CHUNKS, 2, 8, 64, WIDTH)
    dma = pltpu.SemaphoreType.DMA
    return pl.pallas_call(
        kernel,
        out_shape=jax.ShapeDtypeStruct(coefficients.shape, F32),
        in_specs=[
            pl.BlockSpec(memory_space=pltpu.SMEM),
            pl.BlockSpec(memory_space=pltpu.VMEM),
            pl.BlockSpec(memory_space=pltpu.HBM),
            pl.BlockSpec(memory_space=pltpu.HBM),
        ],
        out_specs=pl.BlockSpec(memory_space=pl.ANY),
        scratch_shapes=[
            pltpu.VMEM(state, F32),
            pltpu.VMEM((NODES, RANK, 2 * RANK), F32),
            pltpu.VMEM((7, NODES, RANK, 2 * RANK), F32),
            pltpu.VMEM((HALF, RANK, 2 * RANK), F32),
            pltpu.VMEM((8, NODES, 2 * RANK, 2 * RANK), BF16),
            pltpu.VMEM((NODES, RANK, 2 * WIDTH), BF16),
            pltpu.VMEM((NODES * RANK, 2 * WIDTH), BF16),
            pltpu.VMEM((NODES, RANK, 2 * WIDTH), BF16),
            pltpu.VMEM((NODES, RANK, 2 * WIDTH), BF16),
            pltpu.VMEM((NODES * RANK, NODES * RANK), BF16),
            pltpu.VMEM(state, F32),
            pltpu.VMEM(state, F32),
            pltpu.VMEM(state, F32),
            pltpu.VMEM(state, F32),
            pltpu.VMEM(halves, F32),
            pltpu.VMEM(halves, F32),
            pltpu.VMEM((CHUNKS, HALF, RANK, WIDTH), F32),
            pltpu.VMEM(state, F32),
            pltpu.VMEM(state, F32),
            pltpu.VMEM(state, F32),
            pltpu.VMEM(state, F32),
            pltpu.SMEM((6, NODES), jnp.int32),
            dma((2,)),
            dma((CHUNKS,)),
            dma,
            dma,
            dma((CHUNKS, NODES)),
            dma((CHUNKS, NODES)),
            dma((CHUNKS, NODES)),
            dma((CHUNKS, NODES)),
            dma((CHUNKS, NODES)),
            dma((CHUNKS, NODES)),
            dma((CHUNKS, HALF)),
            dma((CHUNKS, HALF)),
            dma((CHUNKS, NODES)),
            dma((CHUNKS, NODES)),
            dma((CHUNKS, 2)),
        ],
        compiler_params=pltpu.CompilerParams(
            collective_id=1, has_side_effects=True, vmem_limit_bytes=50 * 2**20
        ),
    )(local_bits, relabel.reshape(8, 128), coefficients, transfer)


def solution(mesh):
    placed = (P(("src", "tgt"), None, None), P(None, ("src", "tgt"), None, None), P(), P())
    return jax.shard_map(
        on_device,
        mesh=mesh,
        in_specs=placed,
        out_specs=P(("src", "tgt"), None, None),
        check_vma=False,
    )
```
